32 devices in a mesh: dp: 4 (over y, core), wide: 8 (over z, x).
Axes of the slice: x: 2, y: 2, z: 4, core: 2. Of those that a mesh axis runs over, the one named last changes fastest.
Arguments:
- frames: bfloat16 [4, 2, 16, 64, 512], P('dp', None, 'wide'), may hold values from -6 to 6
- conv_weight: bfloat16 [3, 512, 512], replicated, may hold values from -0.15625 to 0.15625
- embed_weight: bfloat16 [512, 1536], replicated, may hold values from -0.25 to 0.25
- query_weight: bfloat16 [1536, 1536], P('wide'), may hold values from -3 to 3
- key_weight: bfloat16 [1536, 1536], P('wide'), may hold values from -3 to 3
- value_weight: bfloat16 [1536, 1536], P('wide'), may hold values from -0.15625 to 0.15625
- output_weight: bfloat16 [1536, 1536], P('wide'), may hold values from -0.15625 to 0.15625
- out_grad: bfloat16 [4, 4, 16, 64, 1536], P('dp', None, 'wide'), may hold values from -0.119628906 to 0.119628906
- bucket_owner: int32 [16], replicated, may hold values from 0 to 3, as said below
- clip_bucket: int32 [4, 2], replicated, may hold values from 0 to 15, as said below
- clip_frames: int32 [4, 2], replicated, may hold values from 4 to 16, as said below
- clip_grid: int32 [4, 2, 2], replicated, may hold values from 2 to 32, as said below
Outputs:
- block_out: bfloat16 [4, 4, 16, 64, 1536], P('dp', None, 'wide')
- grad_query: float32 [1536, 1536], P('wide')
- grad_key: float32 [1536, 1536], P('wide')
- grad_value: float32 [1536, 1536], P('wide')
- grad_output: float32 [1536, 1536], P('wide')
The draws below stay inside these ranges and needn't reach their ends.
Inputs may be any that keep to these rules, and one draw needn't show every extreme that they name: `bucket_owner`: each owner has exactly 4 buckets. `clip_bucket`: the 2 clips of one group have buckets of different owners; some owner has a clip of every group. `clip_frames`: some clip has all 16 frames. `clip_grid`: the product of a clip's two entries is at most 64, and equals it for some clip.
All inputs are finite; a program needn't handle non-finite values.
Results may differ from the reference program's by a relative error of at most 0.025.
Values may be sent and summed in bfloat16 or wider, within the bound.
A program may use at most 128 MiB of HBM per device.

```python
import math
import jax
import jax.numpy as jnp
from jax import lax

D = 1536
HEADS = 12
HEAD_DIM = 128
CHANNELS = 512
SITES = 64
FR_DEV = 2
CLIPS = 2
OWNER_BUCKETS = 4
TIME = 16
BUCKETS = 16
N_DP = 4
N_WIDE = 8


def bucket_plan(key):
    base = jax.random.fold_in(key, 11)
    order = jax.random.permutation(jax.random.fold_in(base, 1), BUCKETS)
    owners = order % N_DP
    inverse = jnp.argsort(order)
    last_code = order[BUCKETS - 1]
    anchor = last_code % N_DP
    last_pick = last_code // N_DP

    def one_group(group):
        group_key = jax.random.fold_in(base, 100 + group)
        others = (anchor + 1 + jax.random.permutation(jax.random.fold_in(group_key, 1), N_DP - 1)) % N_DP
        chosen = jnp.concatenate([anchor[None], others])[:CLIPS]
        picked = jax.random.randint(jax.random.fold_in(group_key, 3), (CLIPS,), 0, OWNER_BUCKETS)
        first_pick = jnp.where(group == 0, last_pick, picked[0])
        picked = jnp.concatenate([first_pick[None], picked[1:]])
        buckets = inverse[chosen + N_DP * picked]
        return jax.random.permutation(jax.random.fold_in(group_key, 2), buckets)
    buckets = jax.vmap(one_group)(jnp.arange(N_DP))
    return (owners.astype(jnp.int32), buckets.astype(jnp.int32))


def draw_bucket_owner(key, part):
    return bucket_plan(key)[0]


def draw_clip_bucket(key, part):
    return bucket_plan(key)[1]


def draw_clip_frames(key, part):
    base = jax.random.fold_in(key, 31)
    counts = jax.random.randint(jax.random.fold_in(base, 1), (N_DP * CLIPS,), TIME // 4, TIME + 1)
    chosen = jax.random.randint(jax.random.fold_in(base, 2), (), 0, N_DP * CLIPS)
    counts = jnp.where(jnp.arange(N_DP * CLIPS) == chosen, TIME, counts)
    return counts.reshape(N_DP, CLIPS).astype(jnp.int32)


def draw_clip_grid(key, part):
    base = jax.random.fold_in(key, 37)
    grid_rows = jax.random.randint(jax.random.fold_in(base, 1), (N_DP * CLIPS,), 2, 9)
    trimmed = jax.random.randint(jax.random.fold_in(base, 2), (N_DP * CLIPS,), 0, 2)
    order = jax.random.permutation(jax.random.fold_in(base, 3), N_DP * CLIPS)
    position = jnp.arange(N_DP * CLIPS)
    full_mark = position == order[0]
    tall_mark = position == order[1]
    narrow_mark = position == order[2]
    grid_rows = jnp.where(full_mark, 8, grid_rows)
    trimmed = jnp.where(full_mark, 0, trimmed)
    grid_rows = jnp.where(tall_mark, 2, grid_rows)
    trimmed = jnp.where(tall_mark, 0, trimmed)
    grid_rows = jnp.where(narrow_mark, 8, grid_rows)
    trimmed = jnp.where(narrow_mark, 1, trimmed)
    grid_cols = SITES // grid_rows - trimmed
    return jnp.stack([grid_rows, grid_cols], axis=-1).reshape(N_DP, CLIPS, 2).astype(jnp.int32)


def query_key_base(key):
    base = jax.random.fold_in(key, 47)
    shape = (D, HEADS * HEAD_DIM)
    shared = jnp.clip(jax.random.normal(jax.random.fold_in(base, 1), shape, jnp.float32), -4.0, 4.0)
    other = jnp.clip(jax.random.normal(jax.random.fold_in(base, 2), shape, jnp.float32), -4.0, 4.0)
    return (shared, other)


def draw_query_weight(key, part):
    shared, other = query_key_base(key)
    values = shared
    return (values / math.sqrt(D)).astype(jnp.bfloat16)


def draw_key_weight(key, part):
    shared, other = query_key_base(key)
    values = other
    return (values / math.sqrt(D)).astype(jnp.bfloat16)


def block_levels(own_key, dims, pieces, low, high):
    loudness = 1.0
    for dim, parts in pieces:
        heights = jax.random.uniform(jax.random.fold_in(jax.random.fold_in(own_key, 6), dim), (parts,), jnp.float32, low / len(pieces), high / len(pieces))
        loudness = loudness * jnp.repeat(jnp.exp(heights), dims[dim] // parts).reshape((-1,) + (1,) * (len(dims) - 1 - dim))
    return loudness


def gaussian(rng, shape, scale, bound, cuts=(), kind=jnp.bfloat16):
    result = jax.random.normal(rng, shape, jnp.float32) * scale
    if len(cuts) > 0:
        result = block_levels(rng, shape, cuts, -0.22, 0.18) * result
    return jnp.clip(result, min=-bound, max=bound).astype(kind)


def setup_inputs(seed: int = 0) -> dict:
    key_list = jax.random.split(jax.random.key(seed), 13)
    frames = gaussian(key_list[0], (N_DP, CLIPS, TIME, SITES, CHANNELS), 1.0, 6.0, ((0, 4), (2, 8)))
    conv_weight = gaussian(key_list[1], (3, CHANNELS, CHANNELS), (3 * CHANNELS) ** -0.5, 0.15625)
    embed_weight = gaussian(key_list[2], (CHANNELS, D), CHANNELS ** -0.5, 0.25)
    query_weight = draw_query_weight(jax.random.fold_in(key_list[12], 71), 0)
    key_weight = draw_key_weight(jax.random.fold_in(key_list[12], 71), 0)
    value_weight = gaussian(key_list[5], (D, HEADS * HEAD_DIM), D ** -0.5, 0.15625, ((0, 8),))
    output_weight = gaussian(key_list[6], (HEADS * HEAD_DIM, D), (HEADS * HEAD_DIM) ** -0.5, 0.15625, ((0, 8),))
    out_grad = gaussian(key_list[7], (N_DP, N_DP, TIME, SITES, D), 0.02, 0.119628906, ((0, 4), (2, 8)))
    bucket_owner = draw_bucket_owner(jax.random.fold_in(key_list[12], 71), 0)
    clip_bucket = draw_clip_bucket(jax.random.fold_in(key_list[12], 71), 0)
    clip_frames = draw_clip_frames(jax.random.fold_in(key_list[12], 71), 0)
    clip_grid = draw_clip_grid(jax.random.fold_in(key_list[12], 71), 0)
    return {"frames": frames, "conv_weight": conv_weight, "embed_weight": embed_weight, "query_weight": query_weight, "key_weight": key_weight, "value_weight": value_weight, "output_weight": output_weight, "out_grad": out_grad, "bucket_owner": bucket_owner, "clip_bucket": clip_bucket, "clip_frames": clip_frames, "clip_grid": clip_grid}


EPS = 1e-06
masked_score = -1e+30

def widen(array):
    return lax.optimization_barrier(array).astype(jnp.float32)

def layer_norm(values):
    floats = values.astype(jnp.float32)
    center = floats - lax.optimization_barrier(jnp.mean(floats, axis=-1, keepdims=True))
    spread = lax.optimization_barrier(jnp.mean(center * center, axis=-1, keepdims=True))
    return (center * lax.rsqrt(spread + EPS)).astype(jnp.bfloat16)

def reference(frames, conv_weight, embed_weight, query_weight, key_weight, value_weight, output_weight, out_grad, bucket_owner, clip_bucket, clip_frames, clip_grid):
    scale = 1.0 / math.sqrt(HEAD_DIM)
    active = widen(jax.nn.silu(frames.astype(jnp.float32)).astype(jnp.bfloat16))
    summed = frames.astype(jnp.float32)
    for offset in range(3):
        moved = jnp.pad(active, ((0, 0), (0, 0), (offset, 0), (0, 0), (0, 0)))[:, :, :TIME]
        summed = summed + jnp.einsum('gctsa,ab->gctsb', moved, conv_weight[offset].astype(jnp.float32))
    encoded = summed.astype(jnp.bfloat16)
    embedded = jnp.einsum('gctsa,ad->gctsd', widen(encoded), embed_weight.astype(jnp.float32)).astype(jnp.bfloat16)
    owners = bucket_owner[clip_bucket]
    group_index = jnp.arange(N_DP, dtype=jnp.int32)
    table = (owners[None, :, :] == group_index[:, None, None]).astype(jnp.int32)
    grouped = jnp.einsum('ogc,gctsd->ogtsd', table.astype(jnp.float32), widen(embedded)).astype(jnp.bfloat16)
    live_frames = lax.optimization_barrier(jnp.sum(table * clip_frames[None], axis=-1))
    grid_tokens = clip_grid[..., 0] * clip_grid[..., 1]
    live_tokens = lax.optimization_barrier(jnp.sum(table * grid_tokens[None], axis=-1))
    key_tokens = jnp.where(live_tokens > 0, live_tokens, SITES)
    time_pos = jnp.arange(TIME, dtype=jnp.int32)
    site_pos = jnp.arange(SITES, dtype=jnp.int32)
    live = (time_pos[None, None, :, None] < live_frames[:, :, None, None]) & (site_pos[None, None, None, :] < live_tokens[:, :, None, None])
    normed = layer_norm(widen(grouped))
    head_shape = (N_DP, N_DP, TIME, SITES, HEADS, HEAD_DIM)
    query = jnp.einsum('ogtsd,de->ogtse', widen(normed), query_weight.astype(jnp.float32)).astype(jnp.bfloat16)
    keys = jnp.einsum('ogtsd,de->ogtse', widen(normed), key_weight.astype(jnp.float32)).astype(jnp.bfloat16)
    values = jnp.einsum('ogtsd,de->ogtse', widen(normed), value_weight.astype(jnp.float32)).astype(jnp.bfloat16)
    query_heads = query.reshape(head_shape)
    key_heads = keys.reshape(head_shape)
    value_heads = values.reshape(head_shape)
    scores = jnp.einsum('ogtshd,ogtuhd->ogthsu', widen(query_heads), widen(key_heads)) * scale
    key_mask = site_pos[None, None, :] < key_tokens[:, :, None]
    scores = jnp.where(key_mask[:, :, None, None, None, :], scores, masked_score)
    top = lax.optimization_barrier(jnp.max(scores, axis=-1, keepdims=True))
    weights = jnp.exp(scores - top)
    probs = weights / lax.optimization_barrier(jnp.sum(weights, axis=-1, keepdims=True))
    probs_low = probs.astype(jnp.bfloat16)
    attended = jnp.einsum('ogthsu,ogtuhd->ogtshd', widen(probs_low), widen(value_heads)).astype(jnp.bfloat16)
    attended = attended.reshape(N_DP, N_DP, TIME, SITES, D)
    projected = jnp.einsum('ogtsk,kd->ogtsd', widen(attended), output_weight.astype(jnp.float32))
    block = (widen(grouped) + projected).astype(jnp.bfloat16)
    block_out = jnp.where(live[..., None], block, jnp.zeros((), jnp.bfloat16))
    upstream = jnp.where(live[..., None], out_grad, jnp.zeros((), jnp.bfloat16))
    d_attended = jnp.einsum('ogtsd,kd->ogtsk', upstream.astype(jnp.float32), output_weight.astype(jnp.float32)).astype(jnp.bfloat16)
    d_att_heads = d_attended.reshape(head_shape)
    d_probs = jnp.einsum('ogtshd,ogtuhd->ogthsu', widen(d_att_heads), widen(value_heads))
    inner = lax.optimization_barrier(jnp.sum(probs * d_probs, axis=-1, keepdims=True))
    d_scores = (probs * (d_probs - inner) * scale).astype(jnp.bfloat16)
    d_query = jnp.einsum('ogthsu,ogtuhd->ogtshd', widen(d_scores), widen(key_heads)).astype(jnp.bfloat16).reshape(N_DP, N_DP, TIME, SITES, D)
    d_keys = jnp.einsum('ogthsu,ogtshd->ogtuhd', widen(d_scores), widen(query_heads)).astype(jnp.bfloat16).reshape(N_DP, N_DP, TIME, SITES, D)
    d_values = jnp.einsum('ogthsu,ogtshd->ogtuhd', widen(probs_low), widen(d_att_heads)).astype(jnp.bfloat16).reshape(N_DP, N_DP, TIME, SITES, D)
    pairs = ((normed, d_query), (normed, d_keys), (normed, d_values), (attended, upstream))
    zero_index = jnp.zeros((), jnp.int32)

    def add_block(running, index):
        owner_pos = index // N_WIDE
        slab_pos = index % N_WIDE * FR_DEV
        starts = (owner_pos, zero_index, slab_pos, zero_index, zero_index)
        updated = []
        for accum, pair in zip(running, pairs):
            left_rows = lax.dynamic_slice(pair[0], starts, (1, N_DP, FR_DEV, SITES, D)).reshape(-1, D)
            right_rows = lax.dynamic_slice(pair[1], starts, (1, N_DP, FR_DEV, SITES, D)).reshape(-1, D)
            term = jnp.dot(left_rows.T, right_rows, preferred_element_type=jnp.float32)
            updated.append(accum + widen(term.astype(jnp.bfloat16)))
        return (tuple(updated), None)
    empty = jnp.zeros((D, D), jnp.float32)
    totals, unused = lax.scan(add_block, (empty, empty, empty, empty), jnp.arange(N_DP * N_WIDE, dtype=jnp.int32))
    return (block_out, totals[0], totals[1], totals[2], totals[3])
```

```python
import functools
import math

import jax
import jax.numpy as jnp
from jax import lax
from jax.experimental import pallas as pl
from jax.experimental.pallas import tpu as pltpu
from jax.sharding import PartitionSpec as P

HEAD_DIM = 128
CORES = 2
MESH = pl.DeviceIdType.MESH


EPS = 1e-06
masked_score = -1e30


def from_behind(shard, axis, by):
    count = lax.axis_size(axis)
    pairs = [(i, i + by) for i in range(count) if 0 <= i + by < count]
    return lax.ppermute(shard, axis, pairs)


def layer_norm(values):
    floats = values.astype(jnp.float32)
    center = floats - jnp.mean(floats, axis=-1, keepdims=True)
    spread = jnp.mean(center * center, axis=-1, keepdims=True)
    return (center * lax.rsqrt(spread + EPS)).astype(jnp.bfloat16)


class Place:
    def __init__(self, n_wide):
        self.dp = lax.axis_index("dp")
        self.wide = lax.axis_index("wide")
        self.plane, self.core = self.dp // CORES, self.dp % CORES
        self.level, self.side = self.wide // 2, self.wide % 2
        self.levels = n_wide // 2
        self.sibling = (self.plane * CORES + 1 - self.core, self.wide)
        self.across = ((1 - self.plane) * CORES + self.core, self.wide)
        self.beside = (self.dp, self.level * 2 + 1 - self.side)

    def level_at(self, offset):
        return lax.rem(self.level + offset, self.levels)

    def above(self, offset):
        return (self.dp, self.level_at(offset) * 2 + self.side)

    def greet(self):
        barrier = pltpu.get_barrier_semaphore()
        peers = [self.sibling, self.across, self.beside]
        peers += [self.above(o) for o in range(1, self.levels)]
        for peer in peers:
            pl.semaphore_signal(barrier, inc=1, device_id=peer, device_id_type=MESH)
        pl.semaphore_wait(barrier, len(peers))


def span(start, size):
    return pl.ds(pl.multiple_of(start, size), size)


def remote(src, dst, send, recv, peer):
    return pltpu.make_async_remote_copy(
        src_ref=src, dst_ref=dst, send_sem=send, recv_sem=recv, device_id=peer, device_id_type=MESH
    )


def gather_kernel(n_wide, count, *refs):
    shards, fulls = refs[:count], refs[count : 2 * count]
    local_sem, flat_send, flat_recv, across_send, across_recv, core_send, core_recv = refs[2 * count :]
    here = Place(n_wide)
    rows, width = shards[0].shape
    third = width // (CORES * 3)
    half = here.core * (3 * third)
    flat_cols = pl.ds(pl.multiple_of(half + here.plane * third, third), 2 * third)
    across_cols = pl.ds(pl.multiple_of(half + here.plane * (2 * third), third), third)
    core_cols = pl.ds(pl.multiple_of(half, third), 3 * third)
    levels = here.levels

    def block(offset, other):
        side = 1 - here.side if other else here.side
        return pl.ds(pl.multiple_of((here.level_at(offset) * 2 + side) * rows, rows), rows)

    here.greet()
    pending = []
    own = block(0, 0)
    for k in range(count):
        for offset in range(0, levels):
            peer = here.above(offset) if offset else here.beside
            slot = (k, levels - offset, 0) if offset else (k, 0, 1)
            copy = remote(
                shards[k].at[:, flat_cols],
                fulls[k].at[own, flat_cols],
                flat_send.at[k, 0, offset],
                flat_recv.at[slot],
                peer,
            )
            copy.start()
            pending.append(copy)
    locals_ = []
    for k in range(count):
        copy = pltpu.make_async_copy(shards[k], fulls[k].at[own, :], local_sem.at[k])
        copy.start()
        locals_.append(copy)

    def arrived(k, where, cols, recv):
        view = fulls[k].at[where, cols]
        remote(view, view, local_sem.at[k], recv, here.sibling).wait_recv()

    def finish_core(k):
        for other in range(2):
            for offset in range(1 - other, levels):
                where = block(offset, other)
                peer_cols = pl.ds(
                    pl.multiple_of(half + (1 - here.plane) * (2 * third), third), third
                )
                arrived(k, where, peer_cols, across_recv.at[k, offset, other])
                view = fulls[k].at[where, core_cols]
                copy = remote(
                    view, view, core_send.at[k, offset, other], core_recv.at[k, offset, other], here.sibling
                )
                copy.start()
                pending.append(copy)

    for k in range(count):
        for other in range(2):
            for offset in range(1 - other, levels):
                where = block(offset, other)
                arrived(k, where, flat_cols, flat_recv.at[k, offset, other])
                if not other:
                    view = fulls[k].at[where, flat_cols]
                    copy = remote(
                        view, view, flat_send.at[k, 1, offset], flat_recv.at[k, offset, 1], here.beside
                    )
                    copy.start()
                    pending.append(copy)
                view = fulls[k].at[where, across_cols]
                copy = remote(
                    view, view, across_send.at[k, offset, other], across_recv.at[k, offset, other], here.across
                )
                copy.start()
                pending.append(copy)
        if k:
            finish_core(k - 1)
    finish_core(count - 1)
    sibling_cols = pl.ds(pl.multiple_of((1 - here.core) * (3 * third), third), 3 * third)
    for k in range(count):
        for other in range(2):
            for offset in range(1 - other, levels):
                arrived(k, block(offset, other), sibling_cols, core_recv.at[k, offset, other])
    for copy in locals_:
        copy.wait()
    for copy in pending:
        copy.wait_send()


def gather_weights(n_wide, *shards):
    count = len(shards)
    rows, width = shards[0].shape
    levels = n_wide // 2
    dma = pltpu.SemaphoreType.DMA
    return pl.pallas_call(
        functools.partial(gather_kernel, n_wide, count),
        out_shape=[jax.ShapeDtypeStruct((n_wide * rows, width), s.dtype) for s in shards],
        in_specs=[pl.BlockSpec(memory_space=pltpu.VMEM)] * count,
        out_specs=[pl.BlockSpec(memory_space=pl.ANY)] * count,
        scratch_shapes=[
            dma((count,)),
            dma((count, 2, levels)),
            dma((count, levels, 2)),
            dma((count, levels, 2)),
            dma((count, levels, 2)),
            dma((count, levels, 2)),
            dma((count, levels, 2)),
        ],
        compiler_params=pltpu.CompilerParams(
            collective_id=0, has_side_effects=True, vmem_limit_bytes=16 * 1024 * 1024
        ),
        name="gather_weights",
    )(*shards)


def sum_kernel(n_wide, count, *refs):
    terms, out = refs[:count], refs[count]
    half_buf, third_buf, side_buf, level_buf, pair_out, pair_in, fin_out, fin_in = refs[count + 1 : count + 9]
    core_s, core_r, across_s, across_r, side_s, side_r, level_s, level_r, pair_s, pair_r, fin_s, fin_r = refs[
        count + 9 :
    ]
    here = Place(n_wide)
    levels, _, rows, width = terms[0].shape
    third = width // (CORES * 3)
    f32, bf16 = jnp.float32, jnp.bfloat16

    def cols(start, size):
        return pl.ds(pl.multiple_of(start, third), size)

    mine = cols(here.core * (3 * third), 3 * third)
    theirs = cols((1 - here.core) * (3 * third), 3 * third)
    flat = cols(here.plane * third, 2 * third)
    keep = cols(here.plane * (2 * third), third)
    give = cols((1 - here.plane) * (2 * third), third)
    here.greet()

    core_copies = []
    for k in range(count):
        copy = remote(terms[k].at[:, :, :, theirs], half_buf.at[k], core_s.at[k], core_r.at[k], here.sibling)
        copy.start()
        core_copies.append(copy)
    across_copies, side_copies, level_copies, pair_copies, fin_copies = {}, {}, {}, {}, {}

    def stage_core(k):
        core_copies[k].wait_recv()

        @pl.loop(0, levels * 2)
        def _(i):
            a, b = i // 2, i % 2
            half_buf[k, a, b] = (
                half_buf[k, a, b].astype(f32) + terms[k][a, b, :, mine].astype(f32)
            ).astype(bf16)

        across_copies[k] = remote(
            half_buf.at[k, :, :, :, give], third_buf.at[k], across_s.at[k], across_r.at[k], here.across
        )
        across_copies[k].start()

    def stage_across(k):
        across_copies[k].wait_recv()

        @pl.loop(0, levels * 2)
        def _(i):
            a, b = i // 2, i % 2
            half_buf[k, a, b, :, keep] = (
                half_buf[k, a, b, :, keep].astype(f32) + third_buf[k, a, b].astype(f32)
            ).astype(bf16)

        side_copies[k] = remote(
            half_buf.at[k, :, 1 - here.side, :, flat], side_buf.at[k], side_s.at[k], side_r.at[k], here.beside
        )
        side_copies[k].start()

    def stage_side(k):
        side_copies[k].wait_recv()

        @pl.loop(0, levels)
        def _(a):
            side_buf[k, a] = (
                side_buf[k, a].astype(f32) + half_buf[k, a, here.side, :, flat].astype(f32)
            ).astype(bf16)

        level_copies[k] = []
        for offset in range(1, levels):
            copy = remote(
                side_buf.at[k, here.level_at(offset)],
                level_buf.at[k, offset - 1],
                level_s.at[k, offset - 1],
                level_r.at[k, offset - 1],
                here.above(offset),
            )
            copy.start()
            level_copies[k].append(copy)

    def stage_level(k):
        total = side_buf[k, here.level].astype(f32)
        for offset in range(1, levels):
            level_copies[k][offset - 1].wait_recv()
            total = total + level_buf[k, offset - 1].astype(f32)
        pair_out[k] = total.astype(bf16)
        pair_copies[k] = remote(pair_out.at[k], pair_in.at[k], pair_s.at[k], pair_r.at[k], here.across)
        pair_copies[k].start()

    def stage_pair(k):
        pair_copies[k].wait_recv()
        first, second = cols(0, third), cols(third, third)
        shared_mine = cols((1 - here.plane) * third, third)
        shared_peer = cols(here.plane * third, third)
        shared = pair_out[k, :, shared_mine].astype(f32) + pair_in[k, :, shared_peer].astype(f32)
        fin_out[k, :, second] = shared.astype(bf16)
        fin_out[k, :, keep] = pair_out[k, :, cols(here.plane * third, third)]
        fin_out[k, :, give] = pair_in[k, :, cols((1 - here.plane) * third, third)]
        fin_copies[k] = remote(fin_out.at[k], fin_in.at[k], fin_s.at[k], fin_r.at[k], here.sibling)
        fin_copies[k].start()
        out[k, :, mine] = fin_out[k].astype(f32)

    def stage_fin(k):
        fin_copies[k].wait_recv()
        out[k, :, theirs] = fin_in[k].astype(f32)

    stages = (stage_core, stage_across, stage_side, stage_level, stage_pair, stage_fin)
    for step in range(count + len(stages) - 1):
        for i, stage in enumerate(stages):
            if 0 <= step - i < count:
                stage(step - i)
    for k in range(count):
        for copy in (core_copies[k], across_copies[k], side_copies[k], *level_copies[k], pair_copies[k], fin_copies[k]):
            copy.wait_send()


def sum_terms(n_wide, *terms):
    count = len(terms)
    width = terms[0].shape[-1]
    rows = terms[0].shape[0] // n_wide
    levels = n_wide // 2
    third = width // (CORES * 3)
    dma = pltpu.SemaphoreType.DMA
    bf16 = jnp.bfloat16
    return pl.pallas_call(
        functools.partial(sum_kernel, n_wide, count),
        out_shape=jax.ShapeDtypeStruct((count, rows, width), jnp.float32),
        in_specs=[pl.BlockSpec(memory_space=pltpu.VMEM)] * count,
        out_specs=pl.BlockSpec(memory_space=pltpu.VMEM),
        scratch_shapes=[
            pltpu.VMEM((count, levels, 2, rows, 3 * third), bf16),
            pltpu.VMEM((count, levels, 2, rows, third), bf16),
            pltpu.VMEM((count, levels, rows, 2 * third), bf16),
            pltpu.VMEM((count, levels - 1, rows, 2 * third), bf16),
            pltpu.VMEM((count, rows, 2 * third), bf16),
            pltpu.VMEM((count, rows, 2 * third), bf16),
            pltpu.VMEM((count, rows, 3 * third), bf16),
            pltpu.VMEM((count, rows, 3 * third), bf16),
            *([dma((count,))] * 6),
            *([dma((count, levels - 1))] * 2),
            *([dma((count,))] * 4),
        ],
        compiler_params=pltpu.CompilerParams(
            collective_id=1, has_side_effects=True, vmem_limit_bytes=60 * 1024 * 1024
        ),
        name="sum_terms",
    )(*[t.reshape(levels, 2, rows, width) for t in terms])


def body(
    frames,
    conv_weight,
    embed_weight,
    query_weight,
    key_weight,
    value_weight,
    output_weight,
    out_grad,
    bucket_owner,
    clip_bucket,
    clip_frames,
    clip_grid,
):
    scale = 1.0 / math.sqrt(HEAD_DIM)
    groups = lax.axis_size("dp")
    my_group = lax.axis_index("dp")
    my_slab = lax.axis_index("wide")
    frame_slab = frames[0]
    clip_count, slab_frames, site_count, channels = frame_slab.shape
    model_width = embed_weight.shape[1]
    head_count = model_width // HEAD_DIM
    earlier = from_behind(frame_slab, "wide", 1)
    joined = jnp.concatenate([earlier, frame_slab], axis=1)
    active = jax.nn.silu(joined.astype(jnp.float32)).astype(jnp.bfloat16)
    summed = frame_slab.astype(jnp.float32)
    for offset in range(3):
        moved = active[:, slab_frames - offset : 2 * slab_frames - offset].reshape(-1, channels)
        summed = summed + jnp.dot(
            moved, conv_weight[offset], preferred_element_type=jnp.float32
        ).reshape(summed.shape)
    encoded = summed.astype(jnp.bfloat16)
    bucket_table = (
        clip_bucket[:, :, None] == jnp.arange(bucket_owner.shape[0], dtype=jnp.int32)
    ).astype(jnp.int32)
    owners = jnp.sum(bucket_table * bucket_owner, axis=-1)
    group_index = jnp.arange(groups, dtype=jnp.int32)
    mine = (group_index == my_group).astype(jnp.int32)
    my_owners = jnp.sum(mine[:, None] * owners, axis=0)
    send_table = (my_owners[None, :] == group_index[:, None]).astype(jnp.bfloat16)
    grid_tokens = clip_grid[..., 0] * clip_grid[..., 1]
    live_frames = jnp.sum(mine[:, None] * clip_frames, axis=0)
    live_tokens = jnp.sum(mine[:, None] * grid_tokens, axis=0)
    key_tokens = jnp.where(live_tokens > 0, live_tokens, site_count)
    frame_pos = my_slab * slab_frames + jnp.arange(slab_frames, dtype=jnp.int32)
    site_pos = jnp.arange(site_count, dtype=jnp.int32)
    live = (frame_pos[None, :, None] < live_frames[:, None, None]) & (
        site_pos[None, None, :] < live_tokens[:, None, None]
    )
    live_rows = live.reshape(-1)
    routed_grad = lax.all_to_all(out_grad[0], "dp", split_axis=0, concat_axis=0, tiled=True)
    clip_grad = jnp.stack(
        [lax.dynamic_index_in_dim(routed_grad, my_owners[c], 0, keepdims=False) for c in range(clip_count)]
    )
    tokens = jnp.dot(
        encoded.reshape(-1, channels), embed_weight, preferred_element_type=jnp.float32
    ).astype(jnp.bfloat16)
    normed = layer_norm(tokens)
    n_wide = lax.axis_size("wide")
    query_full, key_full, value_full, output_full = gather_weights(
        n_wide, query_weight, key_weight, value_weight, output_weight
    )
    weight_rows = (query_full, key_full, value_full)
    query, keys, values = tuple(
        (jnp.dot(normed, rows_now, preferred_element_type=jnp.float32) for rows_now in weight_rows)
    )
    head_shape = (clip_count * slab_frames, site_count, head_count, HEAD_DIM)
    query_heads = query.astype(jnp.bfloat16).reshape(head_shape)
    key_heads = keys.astype(jnp.bfloat16).reshape(head_shape)
    value_heads = values.astype(jnp.bfloat16).reshape(head_shape)
    scores = (
        jnp.einsum("bshd,buhd->bhsu", query_heads, key_heads, preferred_element_type=jnp.float32)
        * scale
    )
    key_limit = jnp.repeat(key_tokens, slab_frames)
    key_mask = site_pos[None, :] < key_limit[:, None]
    scores = jnp.where(key_mask[:, None, None, :], scores, masked_score)
    top = jnp.max(scores, axis=-1, keepdims=True)
    weights = jnp.exp(scores - top)
    probs = weights / jnp.sum(weights, axis=-1, keepdims=True)
    probs_low = probs.astype(jnp.bfloat16)
    attended = jnp.einsum(
        "bhsu,buhd->bshd", probs_low, value_heads, preferred_element_type=jnp.float32
    ).astype(jnp.bfloat16)
    attended = attended.reshape(-1, model_width)
    projected = jnp.dot(attended, output_full, preferred_element_type=jnp.float32)
    block = (tokens.astype(jnp.float32) + projected).astype(jnp.bfloat16)
    block = jnp.where(live_rows[:, None], block, jnp.zeros((), jnp.bfloat16))
    block_out = lax.all_to_all(
        jnp.einsum(
            "oc,cfsw->ofsw",
            send_table,
            block.reshape(clip_count, slab_frames, site_count, model_width),
            preferred_element_type=jnp.float32,
        ).astype(jnp.bfloat16),
        "dp",
        split_axis=0,
        concat_axis=0,
        tiled=True,
    )[None]
    upstream = jnp.where(
        live_rows[:, None], clip_grad.reshape(-1, model_width), jnp.zeros((), jnp.bfloat16)
    )
    term_output = jnp.einsum("rk,rd->kd", attended, upstream, preferred_element_type=jnp.float32)
    d_attended = jnp.einsum(
        "rd,kd->rk", upstream, output_full, preferred_element_type=jnp.float32
    ).astype(jnp.bfloat16)
    d_att_heads = d_attended.reshape(head_shape)
    d_probs = jnp.einsum(
        "bshd,buhd->bhsu", d_att_heads, value_heads, preferred_element_type=jnp.float32
    )
    inner = jnp.sum(probs * d_probs, axis=-1, keepdims=True)
    d_scores = (probs * (d_probs - inner) * scale).astype(jnp.bfloat16)
    d_query = (
        jnp.einsum("bhsu,buhd->bshd", d_scores, key_heads, preferred_element_type=jnp.float32)
        .astype(jnp.bfloat16)
        .reshape(-1, model_width)
    )
    d_keys = (
        jnp.einsum("bhsu,bshd->buhd", d_scores, query_heads, preferred_element_type=jnp.float32)
        .astype(jnp.bfloat16)
        .reshape(-1, model_width)
    )
    d_values = (
        jnp.einsum("bhsu,bshd->buhd", probs_low, d_att_heads, preferred_element_type=jnp.float32)
        .astype(jnp.bfloat16)
        .reshape(-1, model_width)
    )
    term_query = jnp.einsum("rk,rd->kd", normed, d_query, preferred_element_type=jnp.float32)
    term_key = jnp.einsum("rk,rd->kd", normed, d_keys, preferred_element_type=jnp.float32)
    term_value = jnp.einsum("rk,rd->kd", normed, d_values, preferred_element_type=jnp.float32)
    totals = sum_terms(
        n_wide,
        *(t.astype(jnp.bfloat16) for t in (term_value, term_key, term_query, term_output)),
    )
    return (block_out, totals[2], totals[1], totals[0], totals[3])


def solution(mesh):
    in_specs = (
        P("dp", None, "wide", None, None),
        P(),
        P(),
        P("wide", None),
        P("wide", None),
        P("wide", None),
        P("wide", None),
        P("dp", None, "wide", None, None),
        P(),
        P(),
        P(),
        P(),
    )
    out_specs = (
        P("dp", None, "wide", None, None),
        P("wide", None),
        P("wide", None),
        P("wide", None),
        P("wide", None),
    )
    return jax.shard_map(body, mesh=mesh, in_specs=in_specs, out_specs=out_specs, check_vma=False)
```

```python
import functools
import math

import jax
import jax.numpy as jnp
from jax import lax
from jax.experimental import pallas as pl
from jax.experimental.pallas import tpu as pltpu
from jax.sharding import PartitionSpec as P

HEAD_DIM = 128
CORES = 2
MESH = pl.DeviceIdType.MESH


EPS = 1e-06
masked_score = -1e30


def from_behind(shard, axis, by):
    count = lax.axis_size(axis)
    pairs = [(i, i + by) for i in range(count) if 0 <= i + by < count]
    return lax.ppermute(shard, axis, pairs)


def layer_norm(values):
    floats = values.astype(jnp.float32)
    center = floats - jnp.mean(floats, axis=-1, keepdims=True)
    spread = jnp.mean(center * center, axis=-1, keepdims=True)
    return (center * lax.rsqrt(spread + EPS)).astype(jnp.bfloat16)


class Place:
    def __init__(self, n_wide):
        self.dp = lax.axis_index("dp")
        self.wide = lax.axis_index("wide")
        self.plane, self.core = self.dp // CORES, self.dp % CORES
        self.level, self.side = self.wide // 2, self.wide % 2
        self.levels = n_wide // 2
        self.sibling = (self.plane * CORES + 1 - self.core, self.wide)
        self.across = ((1 - self.plane) * CORES + self.core, self.wide)
        self.beside = (self.dp, self.level * 2 + 1 - self.side)

    def level_at(self, offset):
        return lax.rem(self.level + offset, self.levels)

    def above(self, offset):
        return (self.dp, self.level_at(offset) * 2 + self.side)

    def greet(self):
        barrier = pltpu.get_barrier_semaphore()
        peers = [self.sibling, self.across, self.beside]
        peers += [self.above(o) for o in range(1, self.levels)]
        for peer in peers:
            pl.semaphore_signal(barrier, inc=1, device_id=peer, device_id_type=MESH)
        pl.semaphore_wait(barrier, len(peers))


def span(start, size):
    return pl.ds(pl.multiple_of(start, size), size)


def remote(src, dst, send, recv, peer):
    return pltpu.make_async_remote_copy(
        src_ref=src, dst_ref=dst, send_sem=send, recv_sem=recv, device_id=peer, device_id_type=MESH
    )


def gather_kernel(n_wide, count, *refs):
    shards, fulls = refs[:count], refs[count : 2 * count]
    local_sem, flat_send, flat_recv, across_send, across_recv, core_send, core_recv = refs[2 * count :]
    here = Place(n_wide)
    rows, width = shards[0].shape
    third = width // (CORES * 3)
    half = here.core * (3 * third)
    flat_cols = pl.ds(pl.multiple_of(half + here.plane * third, third), 2 * third)
    across_cols = pl.ds(pl.multiple_of(half + here.plane * (2 * third), third), third)
    core_cols = pl.ds(pl.multiple_of(half, third), 3 * third)
    levels = here.levels

    def block(offset, other):
        side = 1 - here.side if other else here.side
        return pl.ds(pl.multiple_of((here.level_at(offset) * 2 + side) * rows, rows), rows)

    here.greet()
    pending = []
    own = block(0, 0)
    for k in range(count):
        for offset in range(0, levels):
            peer = here.above(offset) if offset else here.beside
            slot = (k, levels - offset, 0) if offset else (k, 0, 1)
            copy = remote(
                shards[k].at[:, flat_cols],
                fulls[k].at[own, flat_cols],
                flat_send.at[k, 0, offset],
                flat_recv.at[slot],
                peer,
            )
            copy.start()
            pending.append(copy)
    locals_ = []
    for k in range(count):
        copy = pltpu.make_async_copy(shards[k], fulls[k].at[own, :], local_sem.at[k])
        copy.start()
        locals_.append(copy)

    def arrived(k, where, cols, recv):
        view = fulls[k].at[where, cols]
        remote(view, view, local_sem.at[k], recv, here.sibling).wait_recv()

    def finish_core(k):
        for other in range(2):
            for offset in range(1 - other, levels):
                where = block(offset, other)
                peer_cols = pl.ds(
                    pl.multiple_of(half + (1 - here.plane) * (2 * third), third), third
                )
                arrived(k, where, peer_cols, across_recv.at[k, offset, other])
                view = fulls[k].at[where, core_cols]
                copy = remote(
                    view, view, core_send.at[k, offset, other], core_recv.at[k, offset, other], here.sibling
                )
                copy.start()
                pending.append(copy)

    for k in range(count):
        for other in range(2):
            for offset in range(1 - other, levels):
                where = block(offset, other)
                arrived(k, where, flat_cols, flat_recv.at[k, offset, other])
                if not other:
                    view = fulls[k].at[where, flat_cols]
                    copy = remote(
                        view, view, flat_send.at[k, 1, offset], flat_recv.at[k, offset, 1], here.beside
                    )
                    copy.start()
                    pending.append(copy)
                view = fulls[k].at[where, across_cols]
                copy = remote(
                    view, view, across_send.at[k, offset, other], across_recv.at[k, offset, other], here.across
                )
                copy.start()
                pending.append(copy)
        if k:
            finish_core(k - 1)
    finish_core(count - 1)
    sibling_cols = pl.ds(pl.multiple_of((1 - here.core) * (3 * third), third), 3 * third)
    for k in range(count):
        for other in range(2):
            for offset in range(1 - other, levels):
                arrived(k, block(offset, other), sibling_cols, core_recv.at[k, offset, other])
    for copy in locals_:
        copy.wait()
    for copy in pending:
        copy.wait_send()


def gather_weights(n_wide, *shards):
    count = len(shards)
    rows, width = shards[0].shape
    levels = n_wide // 2
    dma = pltpu.SemaphoreType.DMA
    return pl.pallas_call(
        functools.partial(gather_kernel, n_wide, count),
        out_shape=[jax.ShapeDtypeStruct((n_wide * rows, width), s.dtype) for s in shards],
        in_specs=[pl.BlockSpec(memory_space=pltpu.VMEM)] * count,
        out_specs=[pl.BlockSpec(memory_space=pl.ANY)] * count,
        scratch_shapes=[
            dma((count,)),
            dma((count, 2, levels)),
            dma((count, levels, 2)),
            dma((count, levels, 2)),
            dma((count, levels, 2)),
            dma((count, levels, 2)),
            dma((count, levels, 2)),
        ],
        compiler_params=pltpu.CompilerParams(
            collective_id=0, has_side_effects=True, vmem_limit_bytes=16 * 1024 * 1024
        ),
        name="gather_weights",
    )(*shards)


def sum_kernel(n_wide, count, parts, site_count, scale, *refs):
    q_ref, k_ref, v_ref, g_ref, mask_ref, normed_t, attended_t, up_ref = refs[:8]
    outs = refs[8 : 8 + count]
    dq_ref, dk_ref, dv_ref = refs[8 + count : 11 + count]
    send_buf, half_buf, third_buf, side_buf, level_buf, pair_out, pair_in, fin_out, fin_in = refs[
        11 + count : 20 + count
    ]
    core_s, core_r, across_s, across_r, side_s, side_r, level_s, level_r, pair_s, pair_r, fin_s, fin_r = refs[
        20 + count :
    ]
    here = Place(n_wide)
    levels, rows = half_buf.shape[1], half_buf.shape[3]
    tokens, width = q_ref.shape
    heads = width // HEAD_DIM
    third = width // (CORES * 3)
    f32, bf16 = jnp.float32, jnp.bfloat16
    chunks = count * parts
    left = (attended_t, normed_t, normed_t, normed_t)
    right = (up_ref, dv_ref, dk_ref, dq_ref)

    def cols(start, size):
        return pl.ds(pl.multiple_of(start, third), size)

    mine = cols(here.core * (3 * third), 3 * third)
    theirs = cols((1 - here.core) * (3 * third), 3 * third)
    flat = cols(here.plane * third, 2 * third)
    keep = cols(here.plane * (2 * third), third)
    give = cols((1 - here.plane) * (2 * third), third)
    here.greet()

    def term(c, i, where):
        k, part = c // parts, c % parts
        lines = pl.ds(pl.multiple_of(i * (rows * parts) + part * rows, rows), rows)
        return jnp.dot(left[k][lines, :], right[k][:, where], preferred_element_type=f32)

    def attention(first, last):
        @pl.loop(first, last)
        def _(h):
            lanes = pl.ds(pl.multiple_of(h * HEAD_DIM, HEAD_DIM), HEAD_DIM)
            for b in range(tokens // site_count):
                at = pl.ds(b * site_count, site_count)
                q, k, v, g = q_ref[at, lanes], k_ref[at, lanes], v_ref[at, lanes], g_ref[at, lanes]
                wide_dot = lambda x, y: lax.dot_general(
                    x, y, (((1,), (1,)), ((), ())), preferred_element_type=f32
                )
                tall_dot = lambda x, y: lax.dot_general(
                    x, y, (((0,), (0,)), ((), ())), preferred_element_type=f32
                )
                scores = jnp.where(mask_ref[pl.ds(b, 1), :] > 0, wide_dot(q, k) * scale, masked_score)
                weights = jnp.exp(scores - jnp.max(scores, axis=-1, keepdims=True))
                probs = weights / jnp.sum(weights, axis=-1, keepdims=True)
                d_probs = wide_dot(g, v)
                inner = jnp.sum(probs * d_probs, axis=-1, keepdims=True)
                d_scores = (probs * (d_probs - inner) * scale).astype(bf16)
                dq_ref[at, lanes] = jnp.dot(d_scores, k, preferred_element_type=f32).astype(bf16)
                dk_ref[at, lanes] = tall_dot(d_scores, q).astype(bf16)
                dv_ref[at, lanes] = tall_dot(probs.astype(bf16), g).astype(bf16)

    copies = {}

    def launch(name, c, *args):
        copy = remote(*args)
        copy.start()
        copies.setdefault((name, c), []).append(copy)

    def emit(c):
        @pl.loop(0, levels * 2)
        def _(i):
            send_buf[c, i // 2, i % 2] = term(c, i, theirs).astype(bf16)

        launch("core", c, send_buf.at[c], half_buf.at[c], core_s.at[c], core_r.at[c], here.sibling)

    def stage_core(c):
        copies["core", c][0].wait_recv()

        @pl.loop(0, levels * 2)
        def _(i):
            x, y = i // 2, i % 2
            half_buf[c, x, y] = (half_buf[c, x, y].astype(f32) + term(c, i, mine)).astype(bf16)

        launch(
            "across", c, half_buf.at[c, :, :, :, give], third_buf.at[c], across_s.at[c], across_r.at[c], here.across
        )

    def stage_across(c):
        copies["across", c][0].wait_recv()

        @pl.loop(0, levels * 2)
        def _(i):
            x, y = i // 2, i % 2
            half_buf[c, x, y, :, keep] = (
                half_buf[c, x, y, :, keep].astype(f32) + third_buf[c, x, y].astype(f32)
            ).astype(bf16)

        launch(
            "side", c, half_buf.at[c, :, 1 - here.side, :, flat], side_buf.at[c], side_s.at[c], side_r.at[c], here.beside
        )

    def stage_side(c):
        copies["side", c][0].wait_recv()

        @pl.loop(0, levels)
        def _(x):
            side_buf[c, x] = (
                side_buf[c, x].astype(f32) + half_buf[c, x, here.side, :, flat].astype(f32)
            ).astype(bf16)

        for offset in range(1, levels):
            launch(
                "level",
                c,
                side_buf.at[c, here.level_at(offset)],
                level_buf.at[c, offset - 1],
                level_s.at[c, offset - 1],
                level_r.at[c, offset - 1],
                here.above(offset),
            )

    def stage_level(c):
        total = side_buf[c, here.level].astype(f32)
        for offset in range(1, levels):
            copies["level", c][offset - 1].wait_recv()
            total = total + level_buf[c, offset - 1].astype(f32)
        pair_out[c] = total.astype(bf16)
        launch("pair", c, pair_out.at[c], pair_in.at[c], pair_s.at[c], pair_r.at[c], here.across)

    def stage_pair(c):
        copies["pair", c][0].wait_recv()
        shared_mine = cols((1 - here.plane) * third, third)
        shared_peer = cols(here.plane * third, third)
        shared = pair_out[c, :, shared_mine].astype(f32) + pair_in[c, :, shared_peer].astype(f32)
        fin_out[c, :, pl.ds(third, third)] = shared.astype(bf16)
        fin_out[c, :, keep] = pair_out[c, :, shared_peer]
        fin_out[c, :, give] = pair_in[c, :, shared_mine]
        launch("fin", c, fin_out.at[c], fin_in.at[c], fin_s.at[c], fin_r.at[c], here.sibling)
        outs[c // parts][pl.ds(c % parts * rows, rows), mine] = fin_out[c].astype(f32)

    def stage_fin(c):
        copies["fin", c][0].wait_recv()
        outs[c // parts][pl.ds(c % parts * rows, rows), theirs] = fin_in[c].astype(f32)

    for c in range(parts):
        emit(c)
    attention(0, heads // 3)
    stage_core(0)
    attention(heads // 3, heads * 2 // 3)
    if parts > 1:
        stage_core(1)
    stage_across(0)
    attention(heads * 2 // 3, heads)
    done = {(emit, c) for c in range(parts)} | {(stage_core, c) for c in range(parts)} | {(stage_across, 0)}
    stages = (emit, stage_core, stage_across, stage_side, stage_level, stage_pair, stage_fin)
    for step in range(chunks + len(stages) - 1):
        for i, stage in enumerate(stages):
            c = step - i
            if 0 <= c < chunks and (stage, c) not in done:
                stage(c)
    for group in copies.values():
        for copy in group:
            copy.wait_send()


def sum_terms(n_wide, site_count, scale, q, k, v, d_att, mask, normed_t, attended_t, upstream):
    count = 4
    tokens, width = q.shape
    full_rows = width // n_wide
    parts = 2 if full_rows % 32 == 0 else 1
    rows = full_rows // parts
    chunks = count * parts
    levels = n_wide // 2
    third = width // (CORES * 3)
    dma = pltpu.SemaphoreType.DMA
    bf16 = jnp.bfloat16
    return pl.pallas_call(
        functools.partial(sum_kernel, n_wide, count, parts, site_count, scale),
        out_shape=[jax.ShapeDtypeStruct((full_rows, width), jnp.float32)] * count,
        in_specs=[pl.BlockSpec(memory_space=pltpu.VMEM)] * 8,
        out_specs=[pl.BlockSpec(memory_space=pltpu.VMEM)] * count,
        scratch_shapes=[
            *([pltpu.VMEM((tokens, width), bf16)] * 3),
            *([pltpu.VMEM((chunks, levels, 2, rows, 3 * third), bf16)] * 2),
            pltpu.VMEM((chunks, levels, 2, rows, third), bf16),
            pltpu.VMEM((chunks, levels, rows, 2 * third), bf16),
            pltpu.VMEM((chunks, levels - 1, rows, 2 * third), bf16),
            pltpu.VMEM((chunks, rows, 2 * third), bf16),
            pltpu.VMEM((chunks, rows, 2 * third), bf16),
            pltpu.VMEM((chunks, rows, 3 * third), bf16),
            pltpu.VMEM((chunks, rows, 3 * third), bf16),
            *([dma((chunks,))] * 6),
            *([dma((chunks, levels - 1))] * 2),
            *([dma((chunks,))] * 4),
        ],
        compiler_params=pltpu.CompilerParams(
            collective_id=1, has_side_effects=True, vmem_limit_bytes=60 * 1024 * 1024
        ),
        cost_estimate=pl.CostEstimate(
            flops=2 * count * tokens * width * width, bytes_accessed=200_000_000, transcendentals=0
        ),
        name="sum_terms",
    )(q, k, v, d_att, mask, normed_t, attended_t, upstream)


def body(
    frames,
    conv_weight,
    embed_weight,
    query_weight,
    key_weight,
    value_weight,
    output_weight,
    out_grad,
    bucket_owner,
    clip_bucket,
    clip_frames,
    clip_grid,
):
    scale = 1.0 / math.sqrt(HEAD_DIM)
    groups = lax.axis_size("dp")
    my_group = lax.axis_index("dp")
    my_slab = lax.axis_index("wide")
    frame_slab = frames[0]
    clip_count, slab_frames, site_count, channels = frame_slab.shape
    model_width = embed_weight.shape[1]
    head_count = model_width // HEAD_DIM
    earlier = from_behind(frame_slab, "wide", 1)
    joined = jnp.concatenate([earlier, frame_slab], axis=1)
    active = jax.nn.silu(joined.astype(jnp.float32)).astype(jnp.bfloat16)
    summed = frame_slab.astype(jnp.float32)
    for offset in range(3):
        moved = active[:, slab_frames - offset : 2 * slab_frames - offset].reshape(-1, channels)
        summed = summed + jnp.dot(
            moved, conv_weight[offset], preferred_element_type=jnp.float32
        ).reshape(summed.shape)
    encoded = summed.astype(jnp.bfloat16)
    bucket_table = (
        clip_bucket[:, :, None] == jnp.arange(bucket_owner.shape[0], dtype=jnp.int32)
    ).astype(jnp.int32)
    owners = jnp.sum(bucket_table * bucket_owner, axis=-1)
    group_index = jnp.arange(groups, dtype=jnp.int32)
    mine = (group_index == my_group).astype(jnp.int32)
    my_owners = jnp.sum(mine[:, None] * owners, axis=0)
    send_table = (my_owners[None, :] == group_index[:, None]).astype(jnp.bfloat16)
    grid_tokens = clip_grid[..., 0] * clip_grid[..., 1]
    live_frames = jnp.sum(mine[:, None] * clip_frames, axis=0)
    live_tokens = jnp.sum(mine[:, None] * grid_tokens, axis=0)
    key_tokens = jnp.where(live_tokens > 0, live_tokens, site_count)
    frame_pos = my_slab * slab_frames + jnp.arange(slab_frames, dtype=jnp.int32)
    site_pos = jnp.arange(site_count, dtype=jnp.int32)
    live = (frame_pos[None, :, None] < live_frames[:, None, None]) & (
        site_pos[None, None, :] < live_tokens[:, None, None]
    )
    live_rows = live.reshape(-1)
    routed_grad = lax.all_to_all(out_grad[0], "dp", split_axis=0, concat_axis=0, tiled=True)
    clip_grad = jnp.stack(
        [lax.dynamic_index_in_dim(routed_grad, my_owners[c], 0, keepdims=False) for c in range(clip_count)]
    )
    tokens = jnp.dot(
        encoded.reshape(-1, channels), embed_weight, preferred_element_type=jnp.float32
    ).astype(jnp.bfloat16)
    normed = layer_norm(tokens)
    n_wide = lax.axis_size("wide")
    query_full, key_full, value_full, output_full = gather_weights(
        n_wide, query_weight, key_weight, value_weight, output_weight
    )
    weight_rows = (query_full, key_full, value_full)
    query, keys, values = tuple(
        (jnp.dot(normed, rows_now, preferred_element_type=jnp.float32) for rows_now in weight_rows)
    )
    head_shape = (clip_count * slab_frames, site_count, head_count, HEAD_DIM)
    query, keys, values = (a.astype(jnp.bfloat16) for a in (query, keys, values))
    query_heads = query.reshape(head_shape)
    key_heads = keys.reshape(head_shape)
    value_heads = values.reshape(head_shape)
    scores = (
        jnp.einsum("bshd,buhd->bhsu", query_heads, key_heads, preferred_element_type=jnp.float32)
        * scale
    )
    key_limit = jnp.repeat(key_tokens, slab_frames)
    key_mask = site_pos[None, :] < key_limit[:, None]
    scores = jnp.where(key_mask[:, None, None, :], scores, masked_score)
    top = jnp.max(scores, axis=-1, keepdims=True)
    weights = jnp.exp(scores - top)
    probs = weights / jnp.sum(weights, axis=-1, keepdims=True)
    probs_low = probs.astype(jnp.bfloat16)
    attended = jnp.einsum(
        "bhsu,buhd->bshd", probs_low, value_heads, preferred_element_type=jnp.float32
    ).astype(jnp.bfloat16)
    attended = attended.reshape(-1, model_width)
    projected = jnp.dot(attended, output_full, preferred_element_type=jnp.float32)
    block = (tokens.astype(jnp.float32) + projected).astype(jnp.bfloat16)
    block = jnp.where(live_rows[:, None], block, jnp.zeros((), jnp.bfloat16))
    block_out = lax.all_to_all(
        jnp.einsum(
            "oc,cfsw->ofsw",
            send_table,
            block.reshape(clip_count, slab_frames, site_count, model_width),
            preferred_element_type=jnp.float32,
        ).astype(jnp.bfloat16),
        "dp",
        split_axis=0,
        concat_axis=0,
        tiled=True,
    )[None]
    upstream = jnp.where(
        live_rows[:, None], clip_grad.reshape(-1, model_width), jnp.zeros((), jnp.bfloat16)
    )
    d_attended = jnp.einsum(
        "rd,kd->rk", upstream, output_full, preferred_element_type=jnp.float32
    ).astype(jnp.bfloat16)
    totals = sum_terms(
        n_wide,
        site_count,
        scale,
        query,
        keys,
        values,
        d_attended,
        key_mask.astype(jnp.float32),
        normed.T,
        attended.T,
        upstream,
    )
    return (block_out, totals[3], totals[2], totals[1], totals[0])


def solution(mesh):
    in_specs = (
        P("dp", None, "wide", None, None),
        P(),
        P(),
        P("wide", None),
        P("wide", None),
        P("wide", None),
        P("wide", None),
        P("dp", None, "wide", None, None),
        P(),
        P(),
        P(),
        P(),
    )
    out_specs = (
        P("dp", None, "wide", None, None),
        P("wide", None),
        P("wide", None),
        P("wide", None),
        P("wide", None),
    )
    return jax.shard_map(body, mesh=mesh, in_specs=in_specs, out_specs=out_specs, check_vma=False)
```

```python
import functools
import math

import jax
import jax.numpy as jnp
from jax import lax
from jax.experimental import pallas as pl
from jax.experimental.pallas import tpu as pltpu
from jax.sharding import PartitionSpec as P

HEAD_DIM = 128
CORES = 2
MESH = pl.DeviceIdType.MESH


EPS = 1e-06
masked_score = -1e30


def from_behind(shard, axis, by):
    count = lax.axis_size(axis)
    pairs = [(i, i + by) for i in range(count) if 0 <= i + by < count]
    return lax.ppermute(shard, axis, pairs)


def layer_norm(values):
    floats = values.astype(jnp.float32)
    center = floats - jnp.mean(floats, axis=-1, keepdims=True)
    spread = jnp.mean(center * center, axis=-1, keepdims=True)
    return (center * lax.rsqrt(spread + EPS)).astype(jnp.bfloat16)


class Place:
    def __init__(self, n_wide):
        self.dp = lax.axis_index("dp")
        self.wide = lax.axis_index("wide")
        self.plane, self.core = self.dp // CORES, self.dp % CORES
        self.level, self.side = self.wide // 2, self.wide % 2
        self.levels = n_wide // 2
        self.sibling = (self.plane * CORES + 1 - self.core, self.wide)
        self.across = ((1 - self.plane) * CORES + self.core, self.wide)
        self.beside = (self.dp, self.level * 2 + 1 - self.side)

    def level_at(self, offset):
        return lax.rem(self.level + offset, self.levels)

    def above(self, offset):
        return (self.dp, self.level_at(offset) * 2 + self.side)

    def greet(self):
        barrier = pltpu.get_barrier_semaphore()
        peers = [self.sibling, self.across, self.beside]
        peers += [self.above(o) for o in range(1, self.levels)]
        for peer in peers:
            pl.semaphore_signal(barrier, inc=1, device_id=peer, device_id_type=MESH)
        pl.semaphore_wait(barrier, len(peers))


def span(start, size):
    return pl.ds(pl.multiple_of(start, size), size)


def remote(src, dst, send, recv, peer):
    return pltpu.make_async_remote_copy(
        src_ref=src, dst_ref=dst, send_sem=send, recv_sem=recv, device_id=peer, device_id_type=MESH
    )


def gather_kernel(n_wide, count, site_count, scale, *refs):
    shards, normed_ref, mask_ref = refs[:count], refs[count], refs[count + 1]
    results, att_ref = refs[count + 2 : 2 * count + 1], refs[2 * count + 1]
    fulls = (*refs[2 * count + 3 : 3 * count + 2], refs[2 * count + 2])
    local_sem, flat_send, flat_recv, across_send, across_recv, core_send, core_recv = refs[3 * count + 2 :]
    here = Place(n_wide)
    rows, width = shards[0].shape
    third = width // (CORES * 3)
    half = here.core * (3 * third)
    flat_cols = pl.ds(pl.multiple_of(half + here.plane * third, third), 2 * third)
    across_cols = pl.ds(pl.multiple_of(half + here.plane * (2 * third), third), third)
    core_cols = pl.ds(pl.multiple_of(half, third), 3 * third)
    levels = here.levels

    def block(offset, other):
        side = 1 - here.side if other else here.side
        return pl.ds(pl.multiple_of((here.level_at(offset) * 2 + side) * rows, rows), rows)

    here.greet()
    pending = []
    own = block(0, 0)
    for k in range(count):
        for offset in range(0, levels):
            peer = here.above(offset) if offset else here.beside
            slot = (k, levels - offset, 0) if offset else (k, 0, 1)
            copy = remote(
                shards[k].at[:, flat_cols],
                fulls[k].at[own, flat_cols],
                flat_send.at[k, 0, offset],
                flat_recv.at[slot],
                peer,
            )
            copy.start()
            pending.append(copy)
    locals_ = []
    for k in range(count):
        copy = pltpu.make_async_copy(shards[k], fulls[k].at[own, :], local_sem.at[k])
        copy.start()
        locals_.append(copy)

    def arrived(k, where, cols, recv):
        view = fulls[k].at[where, cols]
        remote(view, view, local_sem.at[k], recv, here.sibling).wait_recv()

    def finish_core(k):
        for other in range(2):
            for offset in range(1 - other, levels):
                where = block(offset, other)
                peer_cols = pl.ds(
                    pl.multiple_of(half + (1 - here.plane) * (2 * third), third), third
                )
                arrived(k, where, peer_cols, across_recv.at[k, offset, other])
                view = fulls[k].at[where, core_cols]
                copy = remote(
                    view, view, core_send.at[k, offset, other], core_recv.at[k, offset, other], here.sibling
                )
                copy.start()
                pending.append(copy)

    sibling_cols = pl.ds(pl.multiple_of((1 - here.core) * (3 * third), third), 3 * third)
    f32, bf16 = jnp.float32, jnp.bfloat16

    def complete(k):
        for other in range(2):
            for offset in range(1 - other, levels):
                arrived(k, block(offset, other), sibling_cols, core_recv.at[k, offset, other])
        locals_[k].wait()

    def project(k):
        complete(k)

        @pl.loop(0, width // third)
        def _(i):
            lanes = pl.ds(pl.multiple_of(i * third, third), third)
            results[k][:, lanes] = jnp.dot(
                normed_ref[...], fulls[k][:, lanes], preferred_element_type=f32
            ).astype(bf16)

    def attention():
        q_ref, k_ref, v_ref = results

        @pl.loop(0, width // HEAD_DIM)
        def _(h):
            lanes = pl.ds(pl.multiple_of(h * HEAD_DIM, HEAD_DIM), HEAD_DIM)
            for b in range(normed_ref.shape[0] // site_count):
                at = pl.ds(b * site_count, site_count)
                scores = lax.dot_general(
                    q_ref[at, lanes], k_ref[at, lanes], (((1,), (1,)), ((), ())), preferred_element_type=f32
                )
                scores = jnp.where(mask_ref[pl.ds(b, 1), :] > 0, scores * scale, masked_score)
                weights = jnp.exp(scores - jnp.max(scores, axis=-1, keepdims=True))
                probs = weights / jnp.sum(weights, axis=-1, keepdims=True)
                att_ref[at, lanes] = jnp.dot(
                    probs.astype(bf16), v_ref[at, lanes], preferred_element_type=f32
                ).astype(bf16)

    for k in range(count):
        for other in range(2):
            for offset in range(1 - other, levels):
                where = block(offset, other)
                arrived(k, where, flat_cols, flat_recv.at[k, offset, other])
                if not other:
                    view = fulls[k].at[where, flat_cols]
                    copy = remote(
                        view, view, flat_send.at[k, 1, offset], flat_recv.at[k, offset, 1], here.beside
                    )
                    copy.start()
                    pending.append(copy)
                view = fulls[k].at[where, across_cols]
                copy = remote(
                    view, view, across_send.at[k, offset, other], across_recv.at[k, offset, other], here.across
                )
                copy.start()
                pending.append(copy)
        if k:
            finish_core(k - 1)
        if k > 1:
            project(k - 2)
    finish_core(count - 1)
    project(count - 2)
    attention()
    complete(count - 1)
    for copy in pending:
        copy.wait_send()


def gather_weights(n_wide, site_count, scale, normed, mask, *shards):
    count = len(shards)
    rows, width = shards[0].shape
    levels = n_wide // 2
    dma = pltpu.SemaphoreType.DMA
    vmem = pl.BlockSpec(memory_space=pltpu.VMEM)
    full = (n_wide * rows, width)
    return pl.pallas_call(
        functools.partial(gather_kernel, n_wide, count, site_count, scale),
        out_shape=[jax.ShapeDtypeStruct(normed.shape, normed.dtype)] * count
        + [jax.ShapeDtypeStruct(full, shards[0].dtype)],
        in_specs=[vmem] * (count + 2),
        out_specs=[vmem] * count + [pl.BlockSpec(memory_space=pl.ANY)],
        scratch_shapes=[
            *([pltpu.VMEM(full, shards[0].dtype)] * (count - 1)),
            dma((count,)),
            dma((count, 2, levels)),
            *([dma((count, levels, 2))] * 5),
        ],
        compiler_params=pltpu.CompilerParams(
            collective_id=0, has_side_effects=True, vmem_limit_bytes=40 * 1024 * 1024
        ),
        name="gather_weights",
    )(*shards, normed, mask)


def sum_kernel(n_wide, count, parts, site_count, scale, *refs):
    q_ref, k_ref, v_ref, g_ref, mask_ref, normed_t, attended_t, up_ref = refs[:8]
    outs = refs[8 : 8 + count]
    dq_ref, dk_ref, dv_ref = refs[8 + count : 11 + count]
    send_buf, half_buf, third_buf, side_buf, level_buf, pair_out, pair_in, fin_out, fin_in = refs[
        11 + count : 20 + count
    ]
    core_s, core_r, across_s, across_r, side_s, side_r, level_s, level_r, pair_s, pair_r, fin_s, fin_r = refs[
        20 + count :
    ]
    here = Place(n_wide)
    levels, rows = half_buf.shape[1], half_buf.shape[3]
    tokens, width = q_ref.shape
    heads = width // HEAD_DIM
    third = width // (CORES * 3)
    f32, bf16 = jnp.float32, jnp.bfloat16
    chunks = count * parts
    left = (attended_t, normed_t, normed_t, normed_t)
    right = (up_ref, dv_ref, dk_ref, dq_ref)

    def cols(start, size):
        return pl.ds(pl.multiple_of(start, third), size)

    mine = cols(here.core * (3 * third), 3 * third)
    theirs = cols((1 - here.core) * (3 * third), 3 * third)
    flat = cols(here.plane * third, 2 * third)
    keep = cols(here.plane * (2 * third), third)
    give = cols((1 - here.plane) * (2 * third), third)
    here.greet()

    def term(c, i, where):
        k, part = c // parts, c % parts
        lines = pl.ds(pl.multiple_of(i * (rows * parts) + part * rows, rows), rows)
        return jnp.dot(left[k][lines, :], right[k][:, where], preferred_element_type=f32)

    def attention(first, last):
        @pl.loop(first, last)
        def _(h):
            lanes = pl.ds(pl.multiple_of(h * HEAD_DIM, HEAD_DIM), HEAD_DIM)
            for b in range(tokens // site_count):
                at = pl.ds(b * site_count, site_count)
                q, k, v, g = q_ref[at, lanes], k_ref[at, lanes], v_ref[at, lanes], g_ref[at, lanes]
                wide_dot = lambda x, y: lax.dot_general(
                    x, y, (((1,), (1,)), ((), ())), preferred_element_type=f32
                )
                tall_dot = lambda x, y: lax.dot_general(
                    x, y, (((0,), (0,)), ((), ())), preferred_element_type=f32
                )
                scores = jnp.where(mask_ref[pl.ds(b, 1), :] > 0, wide_dot(q, k) * scale, masked_score)
                weights = jnp.exp(scores - jnp.max(scores, axis=-1, keepdims=True))
                probs = weights / jnp.sum(weights, axis=-1, keepdims=True)
                d_probs = wide_dot(g, v)
                inner = jnp.sum(probs * d_probs, axis=-1, keepdims=True)
                d_scores = (probs * (d_probs - inner) * scale).astype(bf16)
                dq_ref[at, lanes] = jnp.dot(d_scores, k, preferred_element_type=f32).astype(bf16)
                dk_ref[at, lanes] = tall_dot(d_scores, q).astype(bf16)
                dv_ref[at, lanes] = tall_dot(probs.astype(bf16), g).astype(bf16)

    copies = {}

    def launch(name, c, *args):
        copy = remote(*args)
        copy.start()
        copies.setdefault((name, c), []).append(copy)

    def emit(c):
        @pl.loop(0, levels * 2)
        def _(i):
            send_buf[c, i // 2, i % 2] = term(c, i, theirs).astype(bf16)

        launch("core", c, send_buf.at[c], half_buf.at[c], core_s.at[c], core_r.at[c], here.sibling)

    def stage_core(c):
        copies["core", c][0].wait_recv()

        @pl.loop(0, levels * 2)
        def _(i):
            x, y = i // 2, i % 2
            half_buf[c, x, y] = (half_buf[c, x, y].astype(f32) + term(c, i, mine)).astype(bf16)

        launch(
            "across", c, half_buf.at[c, :, :, :, give], third_buf.at[c], across_s.at[c], across_r.at[c], here.across
        )

    def stage_across(c):
        copies["across", c][0].wait_recv()

        @pl.loop(0, levels * 2)
        def _(i):
            x, y = i // 2, i % 2
            half_buf[c, x, y, :, keep] = (
                half_buf[c, x, y, :, keep].astype(f32) + third_buf[c, x, y].astype(f32)
            ).astype(bf16)

        launch(
            "side", c, half_buf.at[c, :, 1 - here.side, :, flat], side_buf.at[c], side_s.at[c], side_r.at[c], here.beside
        )

    def stage_side(c):
        copies["side", c][0].wait_recv()

        @pl.loop(0, levels)
        def _(x):
            side_buf[c, x] = (
                side_buf[c, x].astype(f32) + half_buf[c, x, here.side, :, flat].astype(f32)
            ).astype(bf16)

        for offset in range(1, levels):
            launch(
                "level",
                c,
                side_buf.at[c, here.level_at(offset)],
                level_buf.at[c, offset - 1],
                level_s.at[c, offset - 1],
                level_r.at[c, offset - 1],
                here.above(offset),
            )

    def stage_level(c):
        total = side_buf[c, here.level].astype(f32)
        for offset in range(1, levels):
            copies["level", c][offset - 1].wait_recv()
            total = total + level_buf[c, offset - 1].astype(f32)
        pair_out[c] = total.astype(bf16)
        launch("pair", c, pair_out.at[c], pair_in.at[c], pair_s.at[c], pair_r.at[c], here.across)

    def stage_pair(c):
        copies["pair", c][0].wait_recv()
        shared_mine = cols((1 - here.plane) * third, third)
        shared_peer = cols(here.plane * third, third)
        shared = pair_out[c, :, shared_mine].astype(f32) + pair_in[c, :, shared_peer].astype(f32)
        fin_out[c, :, pl.ds(third, third)] = shared.astype(bf16)
        fin_out[c, :, keep] = pair_out[c, :, shared_peer]
        fin_out[c, :, give] = pair_in[c, :, shared_mine]
        launch("fin", c, fin_out.at[c], fin_in.at[c], fin_s.at[c], fin_r.at[c], here.sibling)
        outs[c // parts][pl.ds(c % parts * rows, rows), mine] = fin_out[c].astype(f32)

    def stage_fin(c):
        copies["fin", c][0].wait_recv()
        outs[c // parts][pl.ds(c % parts * rows, rows), theirs] = fin_in[c].astype(f32)

    for c in range(parts):
        emit(c)
    attention(0, heads // 3)
    stage_core(0)
    attention(heads // 3, heads * 2 // 3)
    if parts > 1:
        stage_core(1)
    stage_across(0)
    attention(heads * 2 // 3, heads)
    done = {(emit, c) for c in range(parts)} | {(stage_core, c) for c in range(parts)} | {(stage_across, 0)}
    stages = (emit, stage_core, stage_across, stage_side, stage_level, stage_pair, stage_fin)
    for step in range(chunks + len(stages) - 1):
        for i, stage in enumerate(stages):
            c = step - i
            if 0 <= c < chunks and (stage, c) not in done:
                stage(c)
    for group in copies.values():
        for copy in group:
            copy.wait_send()


def sum_terms(n_wide, site_count, scale, q, k, v, d_att, mask, normed_t, attended_t, upstream):
    count = 4
    tokens, width = q.shape
    full_rows = width // n_wide
    parts = 2 if full_rows % 32 == 0 else 1
    rows = full_rows // parts
    chunks = count * parts
    levels = n_wide // 2
    third = width // (CORES * 3)
    dma = pltpu.SemaphoreType.DMA
    bf16 = jnp.bfloat16
    return pl.pallas_call(
        functools.partial(sum_kernel, n_wide, count, parts, site_count, scale),
        out_shape=[jax.ShapeDtypeStruct((full_rows, width), jnp.float32)] * count,
        in_specs=[pl.BlockSpec(memory_space=pltpu.VMEM)] * 8,
        out_specs=[pl.BlockSpec(memory_space=pltpu.VMEM)] * count,
        scratch_shapes=[
            *([pltpu.VMEM((tokens, width), bf16)] * 3),
            *([pltpu.VMEM((chunks, levels, 2, rows, 3 * third), bf16)] * 2),
            pltpu.VMEM((chunks, levels, 2, rows, third), bf16),
            pltpu.VMEM((chunks, levels, rows, 2 * third), bf16),
            pltpu.VMEM((chunks, levels - 1, rows, 2 * third), bf16),
            pltpu.VMEM((chunks, rows, 2 * third), bf16),
            pltpu.VMEM((chunks, rows, 2 * third), bf16),
            pltpu.VMEM((chunks, rows, 3 * third), bf16),
            pltpu.VMEM((chunks, rows, 3 * third), bf16),
            *([dma((chunks,))] * 6),
            *([dma((chunks, levels - 1))] * 2),
            *([dma((chunks,))] * 4),
        ],
        compiler_params=pltpu.CompilerParams(
            collective_id=1, has_side_effects=True, vmem_limit_bytes=60 * 1024 * 1024
        ),
        cost_estimate=pl.CostEstimate(
            flops=2 * count * tokens * width * width, bytes_accessed=200_000_000, transcendentals=0
        ),
        name="sum_terms",
    )(q, k, v, d_att, mask, normed_t, attended_t, upstream)


def body(
    frames,
    conv_weight,
    embed_weight,
    query_weight,
    key_weight,
    value_weight,
    output_weight,
    out_grad,
    bucket_owner,
    clip_bucket,
    clip_frames,
    clip_grid,
):
    scale = 1.0 / math.sqrt(HEAD_DIM)
    groups = lax.axis_size("dp")
    my_group = lax.axis_index("dp")
    my_slab = lax.axis_index("wide")
    frame_slab = frames[0]
    clip_count, slab_frames, site_count, channels = frame_slab.shape
    model_width = embed_weight.shape[1]
    earlier = from_behind(frame_slab, "wide", 1)
    joined = jnp.concatenate([earlier, frame_slab], axis=1)
    active = jax.nn.silu(joined.astype(jnp.float32)).astype(jnp.bfloat16)
    summed = frame_slab.astype(jnp.float32)
    for offset in range(3):
        moved = active[:, slab_frames - offset : 2 * slab_frames - offset].reshape(-1, channels)
        summed = summed + jnp.dot(
            moved, conv_weight[offset], preferred_element_type=jnp.float32
        ).reshape(summed.shape)
    encoded = summed.astype(jnp.bfloat16)
    bucket_table = (
        clip_bucket[:, :, None] == jnp.arange(bucket_owner.shape[0], dtype=jnp.int32)
    ).astype(jnp.int32)
    owners = jnp.sum(bucket_table * bucket_owner, axis=-1)
    group_index = jnp.arange(groups, dtype=jnp.int32)
    mine = (group_index == my_group).astype(jnp.int32)
    my_owners = jnp.sum(mine[:, None] * owners, axis=0)
    send_table = (my_owners[None, :] == group_index[:, None]).astype(jnp.bfloat16)
    grid_tokens = clip_grid[..., 0] * clip_grid[..., 1]
    live_frames = jnp.sum(mine[:, None] * clip_frames, axis=0)
    live_tokens = jnp.sum(mine[:, None] * grid_tokens, axis=0)
    key_tokens = jnp.where(live_tokens > 0, live_tokens, site_count)
    frame_pos = my_slab * slab_frames + jnp.arange(slab_frames, dtype=jnp.int32)
    site_pos = jnp.arange(site_count, dtype=jnp.int32)
    live = (frame_pos[None, :, None] < live_frames[:, None, None]) & (
        site_pos[None, None, :] < live_tokens[:, None, None]
    )
    live_rows = live.reshape(-1)
    routed_grad = lax.all_to_all(out_grad[0], "dp", split_axis=0, concat_axis=0, tiled=True)
    clip_grad = jnp.stack(
        [lax.dynamic_index_in_dim(routed_grad, my_owners[c], 0, keepdims=False) for c in range(clip_count)]
    )
    tokens = jnp.dot(
        encoded.reshape(-1, channels), embed_weight, preferred_element_type=jnp.float32
    ).astype(jnp.bfloat16)
    normed = layer_norm(tokens)
    n_wide = lax.axis_size("wide")
    key_limit = jnp.repeat(key_tokens, slab_frames)
    key_mask = (site_pos[None, :] < key_limit[:, None]).astype(jnp.float32)
    query, keys, values, attended, output_full = gather_weights(
        n_wide, site_count, scale, normed, key_mask, query_weight, key_weight, value_weight, output_weight
    )
    projected = jnp.dot(attended, output_full, preferred_element_type=jnp.float32)
    block = (tokens.astype(jnp.float32) + projected).astype(jnp.bfloat16)
    block = jnp.where(live_rows[:, None], block, jnp.zeros((), jnp.bfloat16))
    block_out = lax.all_to_all(
        jnp.einsum(
            "oc,cfsw->ofsw",
            send_table,
            block.reshape(clip_count, slab_frames, site_count, model_width),
            preferred_element_type=jnp.float32,
        ).astype(jnp.bfloat16),
        "dp",
        split_axis=0,
        concat_axis=0,
        tiled=True,
    )[None]
    upstream = jnp.where(
        live_rows[:, None], clip_grad.reshape(-1, model_width), jnp.zeros((), jnp.bfloat16)
    )
    d_attended = jnp.einsum(
        "rd,kd->rk", upstream, output_full, preferred_element_type=jnp.float32
    ).astype(jnp.bfloat16)
    totals = sum_terms(
        n_wide,
        site_count,
        scale,
        query,
        keys,
        values,
        d_attended,
        key_mask,
        normed.T,
        attended.T,
        upstream,
    )
    return (block_out, totals[3], totals[2], totals[1], totals[0])


def solution(mesh):
    in_specs = (
        P("dp", None, "wide", None, None),
        P(),
        P(),
        P("wide", None),
        P("wide", None),
        P("wide", None),
        P("wide", None),
        P("dp", None, "wide", None, None),
        P(),
        P(),
        P(),
        P(),
    )
    out_specs = (
        P("dp", None, "wide", None, None),
        P("wide", None),
        P("wide", None),
        P("wide", None),
        P("wide", None),
    )
    return jax.shard_map(body, mesh=mesh, in_specs=in_specs, out_specs=out_specs, check_vma=False)
```
